128 devices in a mesh: particle: 16 (over y_hi, z, core), slab: 8 (over x, y_lo).
Axes of the slice: x: 4, y: 4 (y_hi: 2, y_lo: 2; y = y_hi * 2 + y_lo), z: 4, core: 2. Of those that a mesh axis runs over, the one named last changes fastest.
Arguments:
- latent: float32 [32, 16, 128, 128], P('particle', None, 'slab'), may hold values from -6 to 6
- ancestors: int32 [4, 32], replicated, may hold values from 0 to 31
- noise: float32 [4, 32, 16, 128, 128], P(None, 'particle', None, 'slab'), may hold values from -6 to 6
- embed_weight: bfloat16 [16, 256], replicated, may hold values from -1.5 to 1.5
- depth_weight: bfloat16 [7, 7, 256], replicated, may hold values from -0.875 to 0.875
- depth_bias: float32 [256], replicated, may hold values from -3 to 3
- norm_gain: float32 [256], replicated, may hold values from 0.5 to 2
- norm_shift: float32 [256], replicated, may hold values from -3 to 3
- inner_weight: bfloat16 [256, 1024], replicated, may hold values from -0.375 to 0.375
- inner_bias: float32 [1024], replicated, may hold values from -3 to 3
- outer_weight: bfloat16 [1024, 256], replicated, may hold values from -0.1875 to 0.1875
- outer_bias: float32 [256], replicated, may hold values from -3 to 3
- head_weight: bfloat16 [256, 16], replicated, may hold values from -0.375 to 0.375
Outputs:
- final_latent: float32 [32, 16, 128, 128], P('particle', None, 'slab')
The draws below stay inside these ranges and needn't reach their ends.
All inputs are finite; a program needn't handle non-finite values.
Results may differ from the reference program's by a relative error of at most 0.0095.
Values may be sent and summed in bfloat16 or wider, within the bound.
No kernel may reach another device: no remote copies, remote signals or barrier semaphores. Data moves between devices by JAX's collectives and lax.ppermute only.
A program may use at most 64 MiB of HBM per device.

```python
import math
import jax
import jax.numpy as jnp
import numpy as np
from jax import lax

CH = 16
C = 256
HID = 1024
W = 128
STEPS = 4
P_SIZE = 32
H = 128


def place_ends(entries, stream_key, least, top_value):
    index_at = [jax.random.randint(jax.random.fold_in(stream_key, axis), (), 0, length) for axis, length in enumerate(entries.shape)]
    longest = entries.shape.index(max(entries.shape))
    neighbour = index_at[:longest] + [(index_at[longest] + 1) % entries.shape[longest]] + index_at[longest + 1:]
    return entries.at[tuple(index_at)].set(least).at[tuple(neighbour)].set(top_value)


def block_scale(own_key, extent, split, low, largest):
    gain = 1.0
    for dim, blocks in split:
        steps = jax.random.uniform(jax.random.fold_in(jax.random.fold_in(own_key, 6), dim), (blocks,), jnp.float32, low / len(split), largest / len(split))
        gain = gain * jnp.repeat(jnp.exp(steps), extent[dim] // blocks).reshape((-1,) + (1,) * (len(extent) - 1 - dim))
    return gain


def rank_table(number_of, skew):
    loads = [(1 << 20) // math.isqrt(rank ** skew) + 1 for rank in range(1, number_of + 1)]
    deviation = 1 + sum(loads) // (1 << 30)
    return np.cumsum(np.array([max(1, weight // deviation) for weight in loads]))


def skewed_ids(own_key, extent, number_of, lean):
    table = rank_table(number_of, lean)
    lot = jax.random.randint(jax.random.fold_in(own_key, 1), extent, 0, int(table[number_of - 1]))
    grade = jnp.searchsorted(jnp.asarray(table, jnp.int32), lot, side="right")
    return jax.random.permutation(jax.random.fold_in(own_key, 2), number_of)[grade].astype(jnp.int32)


def centred(rng, dims, deviation, bound, split=(), kind=jnp.bfloat16):
    loudness = block_scale(rng, dims, split, -0.22, 0.18) if split else 1.0
    values = jax.random.normal(rng, dims, jnp.float32) * deviation * loudness
    return jnp.minimum(jnp.maximum(values, -bound), bound).astype(kind)


def setup_inputs(seed: int = 0) -> dict:
    key_list = jax.random.split(jax.random.key(seed), 14)
    return {
        "latent": centred(key_list[0], (P_SIZE, CH, H, W), 1.0, 6.0, ((0, 16), (2, 8)), jnp.float32),
        "ancestors": place_ends(skewed_ids(key_list[1], (STEPS, P_SIZE), P_SIZE, 2), jax.random.fold_in(key_list[1], 3), 0, P_SIZE - 1).astype(jnp.int32),
        "noise": centred(key_list[2], (STEPS, P_SIZE, CH, H, W), 1.0, 6.0, ((1, 16), (3, 8)), jnp.float32),
        "embed_weight": centred(key_list[3], (CH, C), CH ** -0.5, 1.5),
        "depth_weight": centred(key_list[4], (7, 7, C), 49 ** -0.5, 0.875),
        "depth_bias": centred(key_list[5], (C,), 0.5, 3.0, (), jnp.float32),
        "norm_gain": jnp.clip(jnp.exp(jax.random.uniform(key_list[6], (C,), jnp.float32, math.log(0.5), math.log(2.0))), 0.5, 2.0),
        "norm_shift": centred(key_list[7], (C,), 0.5, 3.0, (), jnp.float32),
        "inner_weight": centred(key_list[8], (C, HID), C ** -0.5, 0.375),
        "inner_bias": centred(key_list[9], (HID,), 0.5, 3.0, (), jnp.float32),
        "outer_weight": centred(key_list[10], (HID, C), HID ** -0.5, 0.1875),
        "outer_bias": centred(key_list[11], (C,), 0.5, 3.0, (), jnp.float32),
        "head_weight": centred(key_list[12], (C, CH), C ** -0.5, 0.375),
    }


def predict_noise(single, embed_weight, depth_weight, depth_bias, norm_gain, norm_shift, inner_weight, inner_bias, outer_weight, outer_bias, head_weight):
    channels, height, width = single.shape
    features = jnp.einsum('chw,cd->hwd', single.astype(jnp.bfloat16).astype(jnp.float32), embed_weight.astype(jnp.float32), precision=lax.Precision.HIGHEST).astype(jnp.bfloat16)
    padded = jnp.pad(features, ((3, 3), (3, 3), (0, 0)))
    total = jnp.zeros(features.shape, jnp.float32)
    for row_off in range(7):
        for col_off in range(7):
            total = total + padded[row_off:row_off + height, col_off:col_off + width].astype(jnp.float32) * depth_weight[row_off, col_off].astype(jnp.float32)
    conv = total + depth_bias
    center = lax.optimization_barrier(jnp.mean(conv, axis=-1, keepdims=True))
    spread = lax.optimization_barrier(jnp.mean((conv - center) ** 2, axis=-1, keepdims=True))
    normed = ((conv - center) * lax.rsqrt(spread + 1e-06) * norm_gain + norm_shift).astype(jnp.bfloat16)
    flat = normed.reshape(height * width, -1).astype(jnp.float32)
    hidden = jax.nn.gelu(jnp.dot(flat, inner_weight.astype(jnp.float32), precision=lax.Precision.HIGHEST) + inner_bias).astype(jnp.bfloat16)
    mixed = jnp.dot(hidden.astype(jnp.float32), outer_weight.astype(jnp.float32), precision=lax.Precision.HIGHEST) + outer_bias
    block = (features.reshape(height * width, -1).astype(jnp.float32) + mixed).astype(jnp.bfloat16)
    predicted = jnp.dot(block.astype(jnp.float32), head_weight.astype(jnp.float32), precision=lax.Precision.HIGHEST)
    return predicted.T.reshape(channels, height, width)

def reference(latent, ancestors, noise, embed_weight, depth_weight, depth_bias, norm_gain, norm_shift, inner_weight, inner_bias, outer_weight, outer_bias, head_weight):

    def network(single):
        return predict_noise(single, embed_weight, depth_weight, depth_bias, norm_gain, norm_shift, inner_weight, inner_bias, outer_weight, outer_bias, head_weight)
    state = latent
    for section in range(STEPS):
        predicted = lax.map(network, state)
        moved = (0.9 - 0.05 * section) * state + 0.6 * predicted + 0.3 * noise[section]
        state = jnp.take(moved, ancestors[section], axis=0)
    return state
```

```python
import functools

import jax
import jax.numpy as jnp
from jax import lax
from jax.experimental import pallas as pl
from jax.experimental.pallas import tpu as pltpu
from jax.sharding import PartitionSpec as P

STEPS = 4
BF = jnp.bfloat16
F32 = jnp.float32
CUBIC = 0.7978845608028654 * 0.044715
SCALE = CUBIC ** (-1.0 / 3.0)
LINEAR = 0.7978845608028654 * SCALE
SRC, PARTICLE, NUMBER = 0, 32, 64
VMEM = pl.BlockSpec(memory_space=pltpu.VMEM)
SMEM = pl.BlockSpec(memory_space=pltpu.SMEM)


def table_kernel(final_count, anc, place, tab, live, slot):
    steps, count = anc.shape
    first = place[1] * final_count

    def clear(q, carry):
        for s in range(steps):
            live[s, q] = 0
            tab[s, SRC + q] = 0
            tab[s, PARTICLE + q] = 0
        return carry

    lax.fori_loop(0, count, clear, 0)

    def mark_last(p, carry):
        live[steps - 1, anc[steps - 1, first + p]] = 1
        return carry

    lax.fori_loop(0, final_count, mark_last, 0)
    for s in range(steps - 2, -1, -1):

        def mark(q, carry, s=s):
            a = anc[s, q]
            live[s, a] = live[s, a] | live[s + 1, q]
            return carry

        lax.fori_loop(0, count, mark, 0)
    for s in range(steps):

        def fill(q, n, s=s):
            slot[s, q] = n
            tab[s, SRC + n] = n if s == 0 else slot[s - 1, anc[s - 1, q]]
            tab[s, PARTICLE + n] = q
            return n + live[s, q]

        tab[s, NUMBER] = lax.fori_loop(0, count, fill, jnp.int32(0))

    def final(p, carry):
        tab[steps, p] = slot[steps - 1, anc[steps - 1, first + p]]
        return carry

    lax.fori_loop(0, final_count, final, 0)


def make_table(ancestors, place, final_count):
    steps, count = ancestors.shape
    return pl.pallas_call(
        functools.partial(table_kernel, final_count),
        out_shape=jax.ShapeDtypeStruct((steps + 1, 128), jnp.int32),
        in_specs=[SMEM, SMEM],
        out_specs=SMEM,
        scratch_shapes=[pltpu.SMEM((steps, count), jnp.int32), pltpu.SMEM((steps, count), jnp.int32)],
        name="table",
    )(ancestors, place)


def shifted(row, off):
    width = row.shape[1]
    if off == 0:
        return row
    zeros = jnp.zeros((row.shape[0], abs(off)), row.dtype)
    if off > 0:
        return jnp.concatenate([row[:, off:], zeros], axis=1)
    return jnp.concatenate([zeros, row[:, : width + off]], axis=1)


def step_kernel(
    step,
    last,
    tab,
    place,
    own_f,
    own_b,
    part,
    side,
    other,
    noise,
    wconv,
    gain,
    shift,
    win,
    bin_,
    wout,
    wskip,
    moved_f,
    moved_b,
    *rest,
):
    low = place[0] == 0
    flip = place[2]
    ready = rest[-1]
    width = own_b.shape[3]
    chunk = 256

    def convolve(t):
        src = tab[step, SRC + t]
        p0, p1, far = part[src, 0], part[src, 1], other[src]
        s0, s1, s2 = side[src, 0], side[src, 1], side[src, 2]
        rows = [
            lax.select(low, s0, far),
            lax.select(low, s1, p0),
            lax.select(low, s2, p1),
            own_b[src, 0],
            own_b[src, 1],
            lax.select(low, p0, s1),
            lax.select(low, p1, s2),
            lax.select(low, far, s0),
        ]
        taps = [[shifted(row, off) for off in range(-3, 4)] for row in rows]
        ones = jnp.ones((16, width), BF)
        stacks = [jnp.concatenate(sum(taps[r : r + 7], []) + [ones], axis=0) for r in range(2)]
        conv = jnp.dot(wconv[...], jnp.concatenate(stacks, axis=1), preferred_element_type=F32)
        spread = jnp.mean(conv * conv, axis=0, keepdims=True)
        return (conv * lax.rsqrt(spread + 1e-06) * gain[...] + shift[...]).astype(BF)

    def finish(t, normed):
        src = tab[step, SRC + t]
        ones = jnp.ones((16, 2 * width), BF)
        center = jnp.concatenate([own_b[src, 0], own_b[src, 1]], axis=1)
        acc = jnp.dot(wskip[...], jnp.concatenate([center, ones], axis=0), preferred_element_type=F32)
        for h in range(0, win.shape[0], chunk):
            y = jnp.dot(win[h : h + chunk], normed, preferred_element_type=F32)
            y = (y + bin_[h : h + chunk]).astype(BF)
            gate = jnp.tanh(y * (y * y + BF(LINEAR))) + BF(1.0)
            acc = acc + jnp.dot(wout[:, h : h + chunk], y * gate, preferred_element_type=F32)
        q = tab[step, PARTICLE + t]
        source = (q // 2) ^ flip
        for r in range(2):
            value = (
                (0.9 - 0.05 * step) * own_f[src, r].astype(F32)
                + acc[:, r * width : (r + 1) * width]
                + 0.3 * noise[source, 1 + step, q % 2, r].astype(F32)
            )
            moved_f[t, r] = value
            moved_b[t, r] = value.astype(BF)

    def body(t, carry):
        normed = ready[...]
        following = convolve(t)
        finish(jnp.maximum(t - 1, 0), normed)
        ready[...] = following
        return carry

    lax.fori_loop(0, tab[step, NUMBER] + 1, body, 0)
    if last:
        final = rest[0]

        def emit(p, carry):
            final[p] = moved_b[tab[step + 1, p ^ (2 * flip)]]
            return carry

        lax.fori_loop(0, final.shape[0], emit, 0)


def run_step(step, last, *operands):
    own_b, wconv = operands[3], operands[8]
    outs = [jax.ShapeDtypeStruct(own_b.shape, F32), jax.ShapeDtypeStruct(own_b.shape, BF)]
    if last:
        outs.append(jax.ShapeDtypeStruct(own_b.shape, BF))
    return pl.pallas_call(
        functools.partial(step_kernel, step, last),
        out_shape=outs,
        in_specs=[SMEM, SMEM] + [VMEM] * (len(operands) - 2),
        out_specs=[VMEM] * len(outs),
        scratch_shapes=[pltpu.VMEM((wconv.shape[0], 2 * own_b.shape[3]), BF)],
        compiler_params=pltpu.CompilerParams(vmem_limit_bytes=40 << 20),
        cost_estimate=pl.CostEstimate(flops=4 << 30, bytes_accessed=4 << 20, transcendentals=0),
        name=f"step{step}",
    )(*operands)


def pack_kernel(tab, place, states, packed):
    def copy(i, carry):
        q = tab[0, PARTICLE + i]
        packed[i] = states[(q // 2) ^ place[2], 0, q % 2]
        return carry

    lax.fori_loop(0, packed.shape[0], copy, 0)


def pack(slots, tab, place, states):
    return pl.pallas_call(
        pack_kernel,
        out_shape=jax.ShapeDtypeStruct((slots,) + states.shape[3:], BF),
        in_specs=[SMEM, SMEM, VMEM],
        out_specs=VMEM,
        name="pack",
    )(tab, place, states)


def high_low(x):
    high = x.astype(BF)
    return high, (x - high.astype(F32)).astype(BF)


def weights(embed, depth, depth_bias, gain, shift, inner, inner_bias, outer, outer_bias, head, pos):
    hp = lax.Precision.HIGHEST
    full = depth.astype(F32)[:, :, None, :] * embed.astype(F32)[None, None]
    dim = full.shape[-1]
    full = full.reshape(-1, dim)
    full = full - jnp.mean(full, axis=-1, keepdims=True)
    bias = depth_bias - jnp.mean(depth_bias)
    bh, bl = high_low(bias)
    wconv = jnp.concatenate([full.astype(BF), bh[None], bl[None], jnp.zeros((14, dim), BF)], axis=0).T
    wide = lambda v, s: jnp.broadcast_to((v * s)[:, None], (v.shape[0], pos))
    head_f = head.astype(F32)
    wout = (jnp.dot(outer.astype(F32), head_f, precision=hp) * (0.3 * SCALE)).astype(BF).T
    wskip = 0.6 * jnp.dot(embed.astype(F32), head_f, precision=hp)
    oh, ol = high_low(0.6 * jnp.dot(outer_bias[None], head_f, precision=hp))
    wskip = jnp.concatenate([wskip.astype(BF), oh, ol, jnp.zeros((14, head.shape[1]), BF)], axis=0).T
    return (
        wconv,
        wide(gain, 1.0 / SCALE),
        wide(shift, 1.0 / SCALE),
        inner.T,
        wide(inner_bias, 1.0 / SCALE),
        wout,
        wskip,
    )


def per_device(latent, ancestors, noise, embed, depth, depth_bias, gain, shift, inner, inner_bias, outer, outer_bias, head):
    here, channels, rows, width = latent.shape
    parts, slabs = lax.axis_size("particle"), lax.axis_size("slab")
    both = ("particle", "slab")
    half = parts // 2
    chips = half // 2
    total = chips * slabs

    def spot(which, chip, core):
        slab, at = divmod(chip, chips)
        at = chips - 1 - at if slab % 2 else at
        return (which * half + 2 * at + core) * slabs + slab

    sides = [
        pair
        for h in range(2)
        for m in range(total - 1)
        for pair in ((spot(h, m, 0), spot(h, m + 1, 0)), (spot(h, m + 1, 1), spot(h, m, 1)))
    ]
    swapped = [(i, i ^ 1) for i in range(parts)]
    members = [
        [[spot(h, chips * k + m, c) for m in range(chips) for c in range(2)] for h in range(2)] for k in range(slabs)
    ]
    columns = [pair[0] + pair[1] for pair in members]
    halves = [group for pair in members for group in pair]

    at = lax.axis_index("particle")
    core = at % 2
    place = jnp.stack([core, at // half, (lax.axis_index("slab") % 2) * (half - 2)]).astype(jnp.int32)
    tab = make_table(ancestors, place, half * here)
    stacked = jnp.concatenate([latent[None].astype(BF), noise.astype(BF)], axis=0)
    each = rows // half
    stacked = stacked.reshape(STEPS + 1, here, channels, half, each, width).transpose(3, 0, 1, 4, 2, 5)
    outgoing = jnp.concatenate([stacked, stacked], axis=0).reshape(parts, -1, width)
    incoming = lax.all_to_all(outgoing, both, split_axis=0, concat_axis=0, axis_index_groups=columns, tiled=True)
    incoming = incoming.reshape(parts, STEPS + 1, here, each, channels, width)
    params = weights(embed, depth, depth_bias, gain, shift, inner, inner_bias, outer, outer_bias, head, each * width)
    own_f = own_b = pack(half * here, tab, place, incoming)
    for step in range(STEPS):
        part = lax.ppermute(own_b, "particle", swapped)
        near = lax.dynamic_slice_in_dim(own_b, 1 - core, 1, axis=1)
        side = lax.ppermute(jnp.concatenate([near, part], axis=1), both, sides)
        other = lax.ppermute(lax.dynamic_index_in_dim(side, 2 - core, axis=1, keepdims=False), "particle", swapped)
        outs = run_step(step, step == STEPS - 1, tab, place, own_f, own_b, part, side, other, incoming, *params)
        own_f, own_b = outs[0], outs[1]
    final = outs[2].reshape(half, -1, width)
    home = lax.all_to_all(final, both, split_axis=0, concat_axis=0, axis_index_groups=halves, tiled=True)
    home = home.reshape(half, here, each, channels, width).transpose(1, 3, 0, 2, 4)
    return home.reshape(here, channels, rows, width).astype(F32)


def solution(mesh):
    in_specs = (
        P("particle", None, "slab", None),
        P(),
        P(None, "particle", None, "slab", None),
    ) + (P(),) * 10
    out_specs = P("particle", None, "slab", None)
    return jax.shard_map(per_device, mesh=mesh, in_specs=in_specs, out_specs=out_specs, check_vma=False)
```

```python
import functools

import jax
import jax.numpy as jnp
from jax import lax
from jax.experimental import pallas as pl
from jax.experimental.pallas import tpu as pltpu
from jax.sharding import PartitionSpec as P


STEPS = 4
BF = jnp.bfloat16
F32 = jnp.float32
CUBIC = 0.7978845608028654 * 0.044715
SCALE = CUBIC ** (-1.0 / 3.0)
LINEAR = 0.7978845608028654 * SCALE
SRC, PARTICLE, NUMBER = 0, 32, 64
VMEM = pl.BlockSpec(memory_space=pltpu.VMEM)
SMEM = pl.BlockSpec(memory_space=pltpu.SMEM)


def table_kernel(final_count, anc, place, tab, live, slot):
    steps, count = anc.shape
    first = place[1] * final_count

    def clear(q, carry):
        for s in range(steps):
            live[s, q] = 0
            tab[s, SRC + q] = 0
            tab[s, PARTICLE + q] = 0
        return carry

    lax.fori_loop(0, count, clear, 0)

    def mark_last(p, carry):
        live[steps - 1, anc[steps - 1, first + p]] = 1
        return carry

    lax.fori_loop(0, final_count, mark_last, 0)
    for s in range(steps - 2, -1, -1):

        def mark(q, carry, s=s):
            a = anc[s, q]
            live[s, a] = live[s, a] | live[s + 1, q]
            return carry

        lax.fori_loop(0, count, mark, 0)
    for s in range(steps):

        def fill(q, n, s=s):
            slot[s, q] = n
            tab[s, SRC + n] = n if s == 0 else slot[s - 1, anc[s - 1, q]]
            tab[s, PARTICLE + n] = q
            return n + live[s, q]

        tab[s, NUMBER] = lax.fori_loop(0, count, fill, jnp.int32(0))

    def final(p, carry):
        tab[steps, p] = slot[steps - 1, anc[steps - 1, first + p]]
        return carry

    lax.fori_loop(0, final_count, final, 0)


def make_table(ancestors, place, final_count):
    steps, count = ancestors.shape
    return pl.pallas_call(
        functools.partial(table_kernel, final_count),
        out_shape=jax.ShapeDtypeStruct((steps + 1, 128), jnp.int32),
        in_specs=[SMEM, SMEM],
        out_specs=SMEM,
        scratch_shapes=[pltpu.SMEM((steps, count), jnp.int32), pltpu.SMEM((steps, count), jnp.int32)],
        name="table",
    )(ancestors, place)


def doubled(x):
    return jnp.concatenate([x, x], axis=1)


def shifted(row, off):
    width = row.shape[1]
    if off == 0:
        return row
    zeros = jnp.zeros((row.shape[0], abs(off)), row.dtype)
    if off > 0:
        return jnp.concatenate([row[:, off:], zeros], axis=1)
    return jnp.concatenate([zeros, row[:, : width + off]], axis=1)


def step_kernel(
    step,
    last,
    tab,
    place,
    own_f,
    own_b,
    part,
    side,
    other,
    noise,
    wconv,
    gain,
    shift,
    win,
    bin_,
    wout,
    wskip,
    bout,
    moved_f,
    moved_b,
    *rest,
):
    low = place[0] == 0
    flip = place[2]
    ready = rest[-1]
    width = own_b.shape[3]
    chunk = 512

    def convolve(t):
        src = tab[step, SRC + t]
        p0, p1, far = part[src, 0], part[src, 1], other[src]
        s0, s1, s2 = side[src, 0], side[src, 1], side[src, 2]
        rows = [
            lax.select(low, s0, far),
            lax.select(low, s1, p0),
            lax.select(low, s2, p1),
            own_b[src, 0],
            own_b[src, 1],
            lax.select(low, p0, s1),
            lax.select(low, p1, s2),
            lax.select(low, far, s0),
        ]
        taps = [[shifted(row, off) for off in range(-3, 4)] for row in rows]
        ones = jnp.ones((16, width), BF)
        stacks = [jnp.concatenate(sum(taps[r : r + 7], []) + [ones], axis=0) for r in range(2)]
        conv = jnp.dot(wconv[...], jnp.concatenate(stacks, axis=1), preferred_element_type=F32)
        spread = jnp.mean(conv * conv, axis=0, keepdims=True)
        return (conv * lax.rsqrt(spread + 1e-06) * doubled(gain[...]) + doubled(shift[...])).astype(BF)

    def finish(t, normed):
        src = tab[step, SRC + t]
        center = jnp.concatenate([own_b[src, 0], own_b[src, 1]], axis=1)
        acc = jnp.dot(wskip[...], center, preferred_element_type=F32) + doubled(bout[...])
        for h in range(0, win.shape[0], chunk):
            y = jnp.dot(win[h : h + chunk], normed, preferred_element_type=F32)
            y = (y + doubled(bin_[h : h + chunk])).astype(BF)
            gate = jnp.tanh(y * (y * y + BF(LINEAR))) + BF(1.0)
            acc = acc + jnp.dot(wout[:, h : h + chunk], y * gate, preferred_element_type=F32)
        q = tab[step, PARTICLE + t]
        source = (q // 2) ^ flip
        values = []
        for r in range(2):
            value = (
                (0.9 - 0.05 * step) * own_f[src, r].astype(F32)
                + acc[:, r * width : (r + 1) * width]
                + 0.3 * noise[source, step - 1 if step else 1, q % 2, r].astype(F32)
            )
            moved_f[t, r] = value
            moved_b[t, r] = value.astype(BF)
            values.append(value)
        if not last:
            rest[0][t, 0] = lax.select(low, values[1], values[0]).astype(BF)

    def body(t, carry):
        normed = ready[...]
        finish(jnp.maximum(t - 1, 0), normed)
        following = convolve(t)
        ready[...] = following
        return carry

    lax.fori_loop(0, tab[step, NUMBER] + 1, body, 0)
    if last:
        final = rest[0]

        def emit(p, carry):
            final[p] = moved_b[tab[step + 1, p ^ (2 * flip)]]
            return carry

        lax.fori_loop(0, final.shape[0], emit, 0)


def run_step(step, last, *operands):
    own_b, wconv = operands[3], operands[8]
    outs = [jax.ShapeDtypeStruct(own_b.shape, F32), jax.ShapeDtypeStruct(own_b.shape, BF)]
    slots, each, channels, width = own_b.shape
    outs.append(jax.ShapeDtypeStruct((slots, each if last else 1, channels, width), BF))
    return pl.pallas_call(
        functools.partial(step_kernel, step, last),
        out_shape=outs,
        in_specs=[SMEM, SMEM] + [VMEM] * (len(operands) - 2),
        out_specs=[VMEM] * len(outs),
        scratch_shapes=[pltpu.VMEM((wconv.shape[0], 2 * own_b.shape[3]), BF)],
        compiler_params=pltpu.CompilerParams(vmem_limit_bytes=16 << 20),
        cost_estimate=pl.CostEstimate(flops=4 << 30, bytes_accessed=4 << 20, transcendentals=0),
    )(*operands)


def pack_kernel(tab, place, states, packed, near):
    def copy(i, carry):
        q = tab[0, PARTICLE + i]
        source = (q // 2) ^ place[2]
        packed[i] = states[source, 0, q % 2]
        near[i, 0] = states[source, 0, q % 2, 1 - place[0]]
        return carry

    lax.fori_loop(0, packed.shape[0], copy, 0)


def pack(slots, tab, place, states):
    return pl.pallas_call(
        pack_kernel,
        out_shape=[jax.ShapeDtypeStruct((slots, n) + states.shape[4:], BF) for n in (states.shape[3], 1)],
        in_specs=[SMEM, SMEM, VMEM],
        out_specs=[VMEM] * 2,
        name="pack",
    )(tab, place, states)


def column(row, lanes):
    return jnp.broadcast_to(row, (lanes, row.shape[1])).T


def across(a, b):
    return lax.dot_general(a, b, (((1,), (1,)), ((), ())), preferred_element_type=F32)


def weights_kernel(
    embed,
    depth,
    depth_bias,
    gain,
    shift,
    inner,
    inner_bias,
    outer,
    outer_bias,
    head_t,
    wconv,
    gain_c,
    shift_c,
    win,
    bin_c,
    wout,
    wskip,
    bout,
):
    dim = embed.shape[1]
    lanes = gain_c.shape[1]
    source = embed[...].astype(F32)
    diag = lax.broadcasted_iota(jnp.int32, (dim, dim), 0) == lax.broadcasted_iota(jnp.int32, (dim, dim), 1)
    eye = diag.astype(F32).astype(BF)
    taps = []
    for i in range(depth.shape[0]):
        line = depth[i].astype(F32)
        for j in range(depth.shape[1]):
            full = source * line[j : j + 1]
            taps.append((full - jnp.mean(full, axis=1, keepdims=True)).astype(BF))
    bias = depth_bias[...] - jnp.mean(depth_bias[...], axis=1, keepdims=True)
    high = bias.astype(BF).astype(F32)
    index = lax.broadcasted_iota(jnp.int32, (16, dim), 0)
    extra = jnp.where(index == 0, high, jnp.where(index == 1, bias - high, 0.0))
    wconv[...] = across(eye, jnp.concatenate(taps + [extra.astype(BF)], axis=0)).astype(BF)
    gain_c[...] = column(gain[...] * (1.0 / SCALE), lanes)
    shift_c[...] = column(shift[...] * (1.0 / SCALE), lanes)
    for h in range(0, inner.shape[1], dim):
        win[h : h + dim] = across(eye, inner[:, h : h + dim]).astype(BF)
        bin_c[h : h + dim] = column(inner_bias[:, h : h + dim] * (1.0 / SCALE), lanes)
        wout[:, h : h + dim] = (across(head_t[...], outer[h : h + dim]) * (0.3 * SCALE)).astype(BF)
    wskip[...] = (across(head_t[...], embed[...]) * 0.6).astype(BF)
    offset = 0.6 * jnp.sum(head_t[...].astype(F32) * outer_bias[...], axis=1, keepdims=True)
    bout[...] = jnp.broadcast_to(offset, bout.shape)


def weights(embed, depth, depth_bias, gain, shift, inner, inner_bias, outer, outer_bias, head, lanes):
    channels, dim = embed.shape
    hidden = inner.shape[1]
    taps = depth.shape[0] * depth.shape[1] * channels + 16
    shapes = [
        ((dim, taps), BF),
        ((dim, lanes), F32),
        ((dim, lanes), F32),
        ((hidden, dim), BF),
        ((hidden, lanes), F32),
        ((channels, hidden), BF),
        ((channels, channels), BF),
        ((channels, lanes), F32),
    ]
    return pl.pallas_call(
        weights_kernel,
        out_shape=[jax.ShapeDtypeStruct(*shape) for shape in shapes],
        in_specs=[VMEM] * 10,
        out_specs=[VMEM] * len(shapes),
        compiler_params=pltpu.CompilerParams(vmem_limit_bytes=16 << 20),
        name="weights",
    )(
        embed,
        depth,
        depth_bias[None],
        gain[None],
        shift[None],
        inner,
        inner_bias[None],
        outer,
        outer_bias[None],
        head.T,
    )


def spread_kernel(each, *refs):
    ins, out = refs[:-1], refs[-1]
    half = out.shape[0] // 2
    rows = half * each
    channels = out.shape[4]
    images = [ref.at[a] for ref in ins for a in range(ref.shape[0])]
    here = out.shape[2]
    for n, image in enumerate(images):
        for r in range(rows):
            tile = image[pl.ds(r, channels, stride=rows), :].astype(BF)
            for h in range(2):
                out[h * half + r // each, n // here, n % here, r % each] = tile


def spread_rows(parts, here, each, *arrays):
    channels, rows, width = arrays[0].shape[1:]
    images = sum(x.shape[0] for x in arrays)
    return pl.pallas_call(
        functools.partial(spread_kernel, each),
        out_shape=jax.ShapeDtypeStruct((parts, images // here, here, each, channels, width), BF),
        in_specs=[VMEM] * len(arrays),
        out_specs=VMEM,
        compiler_params=pltpu.CompilerParams(vmem_limit_bytes=16 << 20),
        name="spread",
    )(*[x.reshape(x.shape[0], channels * rows, width) for x in arrays])


def per_device(latent, ancestors, noise, embed, depth, depth_bias, gain, shift, inner, inner_bias, outer, outer_bias, head):
    here, channels, rows, width = latent.shape
    parts, slabs = lax.axis_size("particle"), lax.axis_size("slab")
    both = ("particle", "slab")
    half = parts // 2
    chips = half // 2
    total = chips * slabs

    def spot(which, chip, core):
        slab, at = divmod(chip, chips)
        at = chips - 1 - at if slab % 2 else at
        return (which * half + 2 * at + core) * slabs + slab

    sides = [
        pair
        for h in range(2)
        for m in range(total - 1)
        for pair in ((spot(h, m, 0), spot(h, m + 1, 0)), (spot(h, m + 1, 1), spot(h, m, 1)))
    ]
    swapped = [(i, i ^ 1) for i in range(parts)]
    members = [
        [[spot(h, chips * k + m, c) for m in range(chips) for c in range(2)] for h in range(2)] for k in range(slabs)
    ]
    columns = [pair[0] + pair[1] for pair in members]
    halves = [group for pair in members for group in pair]

    at = lax.axis_index("particle")
    core = at % 2
    place = jnp.stack([core, at // half, (lax.axis_index("slab") % 2) * (half - 2)]).astype(jnp.int32)
    tab = make_table(ancestors, place, half * here)
    each = rows // half

    def deliver(x):
        x = x.reshape(parts, -1, width)
        x = lax.all_to_all(x, both, split_axis=0, concat_axis=0, axis_index_groups=columns, tiled=True)
        return x.reshape(parts, -1, here, each, channels, width)

    flat = noise.reshape((-1,) + noise.shape[2:])
    params = weights(embed, depth, depth_bias, gain, shift, inner, inner_bias, outer, outer_bias, head, width)
    first = spread_rows(parts, here, each, latent, flat[:here])
    later = spread_rows(parts, here, each, flat[here:])
    first = deliver(first)
    later = deliver(later)
    first, params = lax.optimization_barrier((first, params))
    own_b, near = pack(half * here, tab, place, first)
    own_f = own_b
    for step in range(STEPS):
        part = lax.ppermute(own_b, "particle", swapped)
        side = lax.ppermute(jnp.concatenate([near, part], axis=1), both, sides)
        other = lax.ppermute(lax.dynamic_index_in_dim(side, 2 - core, axis=1, keepdims=False), "particle", swapped)
        drawn = first if step == 0 else later
        outs = run_step(step, step == STEPS - 1, tab, place, own_f, own_b, part, side, other, drawn, *params)
        own_f, own_b, near = outs
    final = near.reshape(half, -1, width)
    home = lax.all_to_all(final, both, split_axis=0, concat_axis=0, axis_index_groups=halves, tiled=True)
    home = home.reshape(half, here, each, channels, width).transpose(1, 3, 0, 2, 4)
    return home.reshape(here, channels, rows, width).astype(F32)


def solution(mesh):
    in_specs = (
        P("particle", None, "slab", None),
        P(),
        P(None, "particle", None, "slab", None),
    ) + (P(),) * 10
    out_specs = P("particle", None, "slab", None)

    return jax.shard_map(per_device, mesh=mesh, in_specs=in_specs, out_specs=out_specs, check_vma=False)
```

```python
import functools

import jax
import jax.numpy as jnp
from jax import lax
from jax.experimental import pallas as pl
from jax.experimental.pallas import tpu as pltpu
from jax.sharding import PartitionSpec as P


STEPS = 4
BF = jnp.bfloat16
F32 = jnp.float32
CUBIC = 0.7978845608028654 * 0.044715
SCALE = CUBIC ** (-1.0 / 3.0)
LINEAR = 0.7978845608028654 * SCALE
SRC, PARTICLE, NUMBER = 0, 32, 64
VMEM = pl.BlockSpec(memory_space=pltpu.VMEM)
SMEM = pl.BlockSpec(memory_space=pltpu.SMEM)


def table_kernel(final_count, anc, place, tab, live, slot):
    steps, count = anc.shape
    first = place[1] * final_count

    def clear(q, carry):
        for s in range(steps):
            live[s, q] = 0
            tab[s, SRC + q] = 0
            tab[s, PARTICLE + q] = 0
        return carry

    lax.fori_loop(0, count, clear, 0)

    def mark_last(p, carry):
        live[steps - 1, anc[steps - 1, first + p]] = 1
        return carry

    lax.fori_loop(0, final_count, mark_last, 0)
    for s in range(steps - 2, -1, -1):

        def mark(q, carry, s=s):
            a = anc[s, q]
            live[s, a] = live[s, a] | live[s + 1, q]
            return carry

        lax.fori_loop(0, count, mark, 0)
    for s in range(steps):

        def fill(q, n, s=s):
            slot[s, q] = n
            tab[s, SRC + n] = n if s == 0 else slot[s - 1, anc[s - 1, q]]
            tab[s, PARTICLE + n] = q
            return n + live[s, q]

        tab[s, NUMBER] = lax.fori_loop(0, count, fill, jnp.int32(0))

    def final(p, carry):
        tab[steps, p] = slot[steps - 1, anc[steps - 1, first + p]]
        return carry

    lax.fori_loop(0, final_count, final, 0)


def make_table(ancestors, place, final_count):
    steps, count = ancestors.shape
    return pl.pallas_call(
        functools.partial(table_kernel, final_count),
        out_shape=jax.ShapeDtypeStruct((steps + 1, 128), jnp.int32),
        in_specs=[SMEM, SMEM],
        out_specs=SMEM,
        scratch_shapes=[pltpu.SMEM((steps, count), jnp.int32), pltpu.SMEM((steps, count), jnp.int32)],
        name="table",
    )(ancestors, place)


def doubled(x):
    return jnp.concatenate([x, x], axis=1)


def shifted(row, off):
    width = row.shape[1]
    if off == 0:
        return row
    zeros = jnp.zeros((row.shape[0], abs(off)), row.dtype)
    if off > 0:
        return jnp.concatenate([row[:, off:], zeros], axis=1)
    return jnp.concatenate([zeros, row[:, : width + off]], axis=1)


def step_kernel(
    step,
    last,
    tab,
    place,
    own_b,
    part,
    side,
    other,
    noise,
    wconv,
    gain,
    shift,
    win,
    bin_,
    wout,
    wskip,
    bout,
    moved_b,
    *rest,
):
    low = place[0] == 0
    flip = place[2]
    ready = rest[-1]
    width = own_b.shape[3]
    chunk = 512

    def convolve(t):
        src = tab[step, SRC + t]
        p0, p1, far = part[src, 0], part[src, 1], other[src]
        s0, s1, s2 = side[src, 0], side[src, 1], side[src, 2]
        rows = [
            lax.select(low, s0, far),
            lax.select(low, s1, p0),
            lax.select(low, s2, p1),
            own_b[src, 0],
            own_b[src, 1],
            lax.select(low, p0, s1),
            lax.select(low, p1, s2),
            lax.select(low, far, s0),
        ]
        taps = [[shifted(row, off) for off in range(-3, 4)] for row in rows]
        ones = jnp.ones((16, width), BF)
        stacks = [jnp.concatenate(sum(taps[r : r + 7], []) + [ones], axis=0) for r in range(2)]
        conv = jnp.dot(wconv[...], jnp.concatenate(stacks, axis=1), preferred_element_type=F32)
        spread = jnp.mean(conv * conv, axis=0, keepdims=True)
        return (conv * lax.rsqrt(spread + 1e-06) * doubled(gain[...]) + doubled(shift[...])).astype(BF)

    def finish(t, normed):
        src = tab[step, SRC + t]
        center = jnp.concatenate([own_b[src, 0], own_b[src, 1]], axis=1)
        acc = jnp.dot(wskip[...], center, preferred_element_type=F32) + doubled(bout[...])
        for h in range(0, win.shape[0], chunk):
            y = jnp.dot(win[h : h + chunk], normed, preferred_element_type=F32)
            y = (y + doubled(bin_[h : h + chunk])).astype(BF)
            gate = jnp.tanh(y * (y * y + BF(LINEAR))) + BF(1.0)
            acc = acc + jnp.dot(wout[:, h : h + chunk], y * gate, preferred_element_type=F32)
        q = tab[step, PARTICLE + t]
        source = (q // 2) ^ flip
        values = []
        for r in range(2):
            value = (
                (0.9 - 0.05 * step) * own_b[src, r].astype(F32)
                + acc[:, r * width : (r + 1) * width]
                + 0.3 * noise[source, step - 1 if step else 1, q % 2, r].astype(F32)
            )
            moved_b[t, r] = value.astype(BF)
            values.append(value)
        if not last:
            rest[0][t, 0] = lax.select(low, values[1], values[0]).astype(BF)

    def body(t, carry):
        finish(t - 1, ready[...])
        ready[...] = convolve(t)
        return carry

    ready[...] = convolve(0)
    lax.fori_loop(1, tab[step, NUMBER], body, 0)
    finish(tab[step, NUMBER] - 1, ready[...])
    if last:
        final = rest[0]

        def emit(p, carry):
            final[p] = moved_b[tab[step + 1, p ^ (2 * flip)]]
            return carry

        lax.fori_loop(0, final.shape[0], emit, 0)


def run_step(step, last, *operands):
    own_b, wconv = operands[2], operands[7]
    outs = [jax.ShapeDtypeStruct(own_b.shape, BF)]
    slots, each, channels, width = own_b.shape
    outs.append(jax.ShapeDtypeStruct((slots, each if last else 1, channels, width), BF))
    return pl.pallas_call(
        functools.partial(step_kernel, step, last),
        out_shape=outs,
        in_specs=[SMEM, SMEM] + [VMEM] * (len(operands) - 2),
        out_specs=[VMEM] * len(outs),
        scratch_shapes=[pltpu.VMEM((wconv.shape[0], 2 * own_b.shape[3]), BF)],
        compiler_params=pltpu.CompilerParams(vmem_limit_bytes=16 << 20),
        cost_estimate=pl.CostEstimate(flops=4 << 30, bytes_accessed=4 << 20, transcendentals=0),
    )(*operands)


def pack_kernel(tab, place, states, packed, near):
    def copy(i, carry):
        q = tab[0, PARTICLE + i]
        source = (q // 2) ^ place[2]
        packed[i] = states[source, 0, q % 2]
        near[i, 0] = states[source, 0, q % 2, 1 - place[0]]
        return carry

    lax.fori_loop(0, packed.shape[0], copy, 0)


def pack(slots, tab, place, states):
    return pl.pallas_call(
        pack_kernel,
        out_shape=[jax.ShapeDtypeStruct((slots, n) + states.shape[4:], BF) for n in (states.shape[3], 1)],
        in_specs=[SMEM, SMEM, VMEM],
        out_specs=[VMEM] * 2,
        name="pack",
    )(tab, place, states)


def column(row, lanes):
    return jnp.broadcast_to(row, (lanes, row.shape[1])).T


def across(a, b):
    return lax.dot_general(a, b, (((1,), (1,)), ((), ())), preferred_element_type=F32)


def weights_kernel(
    embed,
    depth,
    depth_bias,
    gain,
    shift,
    inner,
    inner_bias,
    outer,
    outer_bias,
    head_t,
    wconv,
    gain_c,
    shift_c,
    win,
    bin_c,
    wout,
    wskip,
    bout,
):
    dim = embed.shape[1]
    lanes = gain_c.shape[1]
    source = embed[...].astype(F32)
    diag = lax.broadcasted_iota(jnp.int32, (dim, dim), 0) == lax.broadcasted_iota(jnp.int32, (dim, dim), 1)
    eye = diag.astype(F32).astype(BF)
    taps = []
    for i in range(depth.shape[0]):
        line = depth[i].astype(F32)
        for j in range(depth.shape[1]):
            full = source * line[j : j + 1]
            taps.append((full - jnp.mean(full, axis=1, keepdims=True)).astype(BF))
    bias = depth_bias[...] - jnp.mean(depth_bias[...], axis=1, keepdims=True)
    high = bias.astype(BF).astype(F32)
    index = lax.broadcasted_iota(jnp.int32, (16, dim), 0)
    extra = jnp.where(index == 0, high, jnp.where(index == 1, bias - high, 0.0))
    wconv[...] = across(eye, jnp.concatenate(taps + [extra.astype(BF)], axis=0)).astype(BF)
    gain_c[...] = column(gain[...] * (1.0 / SCALE), lanes)
    shift_c[...] = column(shift[...] * (1.0 / SCALE), lanes)
    for h in range(0, inner.shape[1], dim):
        win[h : h + dim] = across(eye, inner[:, h : h + dim]).astype(BF)
        bin_c[h : h + dim] = column(inner_bias[:, h : h + dim] * (1.0 / SCALE), lanes)
        wout[:, h : h + dim] = (across(head_t[...], outer[h : h + dim]) * (0.3 * SCALE)).astype(BF)
    wskip[...] = (across(head_t[...], embed[...]) * 0.6).astype(BF)
    offset = 0.6 * jnp.sum(head_t[...].astype(F32) * outer_bias[...], axis=1, keepdims=True)
    bout[...] = jnp.broadcast_to(offset, bout.shape)


def weights(embed, depth, depth_bias, gain, shift, inner, inner_bias, outer, outer_bias, head, lanes):
    channels, dim = embed.shape
    hidden = inner.shape[1]
    taps = depth.shape[0] * depth.shape[1] * channels + 16
    shapes = [
        ((dim, taps), BF),
        ((dim, lanes), F32),
        ((dim, lanes), F32),
        ((hidden, dim), BF),
        ((hidden, lanes), F32),
        ((channels, hidden), BF),
        ((channels, channels), BF),
        ((channels, lanes), F32),
    ]
    return pl.pallas_call(
        weights_kernel,
        out_shape=[jax.ShapeDtypeStruct(*shape) for shape in shapes],
        in_specs=[VMEM] * 10,
        out_specs=[VMEM] * len(shapes),
        compiler_params=pltpu.CompilerParams(vmem_limit_bytes=16 << 20),
        name="weights",
    )(
        embed,
        depth,
        depth_bias[None],
        gain[None],
        shift[None],
        inner,
        inner_bias[None],
        outer,
        outer_bias[None],
        head.T,
    )


def spread_kernel(each, *refs):
    ins, out = refs[:-1], refs[-1]
    half = out.shape[0] // 2
    channels = out.shape[4]
    rows = half * each
    for n, ref in enumerate(ins):
        for j in range(ref.shape[0]):
            for r in range(rows):
                tile = ref[j, pl.ds(r, channels, stride=rows), :].astype(BF)
                for h in range(2):
                    out[h * half + r // each, n, j, r % each] = tile


def spread_rows(parts, here, each, times, *arrays):
    channels, rows, width = arrays[0][0].shape[1:]
    block = (here, channels * rows, width)
    out = (parts, len(arrays), here, each, channels, width)
    return pl.pallas_call(
        functools.partial(spread_kernel, each),
        grid=(times,),
        out_shape=jax.ShapeDtypeStruct((parts, times * len(arrays)) + out[2:], BF),
        in_specs=[pl.BlockSpec(block, lambda i, at=at: (i + at, 0, 0)) for _, at in arrays],
        out_specs=pl.BlockSpec(out, lambda i: (0, i, 0, 0, 0, 0)),
        compiler_params=pltpu.CompilerParams(vmem_limit_bytes=16 << 20),
        name="spread",
    )(*[pltpu.with_memory_space_constraint(x.reshape(x.shape[0], channels * rows, width), pltpu.HBM) for x, _ in arrays])


def per_device(latent, ancestors, noise, embed, depth, depth_bias, gain, shift, inner, inner_bias, outer, outer_bias, head):
    here, channels, rows, width = latent.shape
    parts, slabs = lax.axis_size("particle"), lax.axis_size("slab")
    both = ("particle", "slab")
    half = parts // 2
    chips = half // 2
    total = chips * slabs

    def spot(which, chip, core):
        slab, at = divmod(chip, chips)
        at = chips - 1 - at if slab % 2 else at
        return (which * half + 2 * at + core) * slabs + slab

    sides = [
        pair
        for h in range(2)
        for m in range(total - 1)
        for pair in ((spot(h, m, 0), spot(h, m + 1, 0)), (spot(h, m + 1, 1), spot(h, m, 1)))
    ]
    swapped = [(i, i ^ 1) for i in range(parts)]
    members = [
        [[spot(h, chips * k + m, c) for m in range(chips) for c in range(2)] for h in range(2)] for k in range(slabs)
    ]
    columns = [pair[0] + pair[1] for pair in members]
    halves = [group for pair in members for group in pair]

    at = lax.axis_index("particle")
    core = at % 2
    place = jnp.stack([core, at // half, (lax.axis_index("slab") % 2) * (half - 2)]).astype(jnp.int32)
    tab = make_table(ancestors, place, half * here)
    each = rows // half

    def deliver(x):
        x = x.reshape(parts, -1, width)
        x = lax.all_to_all(x, both, split_axis=0, concat_axis=0, axis_index_groups=columns, tiled=True)
        return x.reshape(parts, -1, here, each, channels, width)

    flat = noise.reshape((-1,) + noise.shape[2:])
    params = weights(embed, depth, depth_bias, gain, shift, inner, inner_bias, outer, outer_bias, head, width)
    first = spread_rows(parts, here, each, 1, (latent, 0), (flat, 0))
    later = spread_rows(parts, here, each, STEPS - 1, (flat, 1))
    first = deliver(first)
    later = deliver(later)
    own_b, near = pack(half * here, tab, place, first)
    for step in range(STEPS):
        part = lax.ppermute(own_b, "particle", swapped)
        side = lax.ppermute(jnp.concatenate([near, part], axis=1), both, sides)
        other = lax.ppermute(lax.dynamic_index_in_dim(side, 2 - core, axis=1, keepdims=False), "particle", swapped)
        drawn = first if step == 0 else later
        outs = run_step(step, step == STEPS - 1, tab, place, own_b, part, side, other, drawn, *params)
        own_b, near = outs
    final = near.reshape(half, -1, width)
    home = lax.all_to_all(final, both, split_axis=0, concat_axis=0, axis_index_groups=halves, tiled=True)
    home = home.reshape(half, here, each, channels, width).transpose(1, 3, 0, 2, 4)
    return home.reshape(here, channels, rows, width).astype(F32)


def solution(mesh):
    in_specs = (
        P("particle", None, "slab", None),
        P(),
        P(None, "particle", None, "slab", None),
    ) + (P(),) * 10
    out_specs = P("particle", None, "slab", None)

    return jax.shard_map(per_device, mesh=mesh, in_specs=in_specs, out_specs=out_specs, check_vma=False)
```
